32 devices in a mesh: dp: 4 (over z), expert: 8 (over y, x, core).
Axes of the slice: x: 2, y: 2, z: 4, core: 2. Of those that a mesh axis runs over, the one named last changes fastest.
Arguments:
- tokens: bfloat16 [4096, 2048], P(('dp', 'expert')), may hold values from -6 to 6
- cotangent: bfloat16 [4096, 2048], P(('dp', 'expert')), may hold values from -1.1953125 to 1.1953125
- expert_ids: int32 [4096, 8], P(('dp', 'expert')), may hold values from 0 to 15, all different within a row; in each aligned block of 128 rows (0 to 127, 128 to 255, ...) at most 80 rows name the same one
- route_weight: float32 [4096, 8], P(('dp', 'expert')), may hold values from 0.02 to 0.3
- gate_proj: bfloat16 [16, 2048, 384], P('expert'), may hold values from -0.125 to 0.125
- up_proj: bfloat16 [16, 2048, 384], P('expert'), may hold values from -0.125 to 0.125
- down_proj: bfloat16 [16, 384, 2048], P('expert'), may hold values from -0.3125 to 0.3125
Outputs:
- layer_out: bfloat16 [4096, 2048], P(('dp', 'expert'))
- route_grad: float32 [4096, 8], P(('dp', 'expert'))
- gate_grad: bfloat16 [16, 2048, 384], P('expert', 'dp')
- up_grad: bfloat16 [16, 2048, 384], P('expert', 'dp')
- down_grad: bfloat16 [16, 384, 2048], P('expert', None, 'dp')
The draws below stay inside these ranges and needn't reach their ends.
Inputs may be any that keep to these rules, and one draw needn't show every extreme that they name: `expert_ids`: each token names 8 different experts. Within the 128 tokens of one device (aligned blocks of rows), no expert is named by more than 80 tokens, a bound that some block reaches.
All inputs are finite; a program needn't handle non-finite values.
Results may differ from the reference program's by a relative error of at most 0.017.
Values may be sent and summed in bfloat16 or wider, within the bound.
No kernel may reach another device: no remote copies, remote signals or barrier semaphores. Data moves between devices by JAX's collectives and lax.ppermute only.
A program may use at most 128 MiB of HBM per device.

```python
import math
import jax
import jax.numpy as jnp
import numpy as np
from jax import lax

D = 2048
FF = 384
TOP = 8
TOK_DEV = 128
EXPERTS = 16
CAP = 80
TOKENS = 4096
N_DP = 4
N_EXPERT = 8


def block_levels(own_key, extent, pieces, least, top_value):
    factor_of, own = 1.0, jax.random.fold_in(own_key, 6)
    for dim, blocks in pieces:
        heights = jnp.exp(jax.random.uniform(jax.random.fold_in(own, dim), (blocks,), jnp.float32, least / len(pieces), top_value / len(pieces)))
        factor_of = factor_of * jnp.repeat(heights, extent[dim] // blocks).reshape([-1 if axis == dim else 1 for axis in range(len(extent))])
    return factor_of


def shared_out(stream_key, own, number, rows, amount, top, limit, lean):
    order = jax.random.permutation(stream_key, amount)
    heavy_load, usual = portions_of(amount, rows * top, limit, lean, True), portions_of(amount, rows * top, limit, lean, False)
    places = jnp.arange(amount)

    def named(sizes, rotation):
        used = int((sizes > 0).sum())
        fixed = max(1, used // 4)
        moved = fixed + (places - fixed + rotation * (used - fixed)) % max(1, amount - fixed)
        return jnp.zeros((amount,), jnp.int32).at[order[jnp.where(places < fixed, places, moved)]].set(jnp.asarray(sizes, jnp.int32))

    sizes = jnp.where(number % 4 == 0, named(heavy_load, number // 4), named(usual, number - number // 4 - 1))
    mixed = jax.random.permutation(jax.random.fold_in(own, 3), amount)
    source_of, sink = mixed[0:amount // 2 * 2:2], mixed[1:amount // 2 * 2:2]
    slack = jnp.minimum(sizes[source_of] - 1, limit - sizes[sink]) // 2
    slack = jnp.where((source_of == order[0]) | (sink == order[0]) | (sizes[sink] == 0), 0, jnp.maximum(slack, 0))
    moved = jax.random.randint(jax.random.fold_in(own, 4), (amount // 2,), 0, 1 << 20) % (slack + 1)
    sizes = sizes.at[source_of].add(-moved).at[sink].add(moved)
    items = jnp.searchsorted(jnp.cumsum(sizes), jnp.arange(rows * top), side="right").astype(jnp.int32)
    table = items.reshape(top, rows).T
    table = table[jax.random.permutation(jax.random.fold_in(own, 1), rows)]
    rotation = jax.random.randint(jax.random.fold_in(own, 2), (rows, 1), 0, top)
    return jnp.take_along_axis(table, (jnp.arange(top)[None, :] + rotation) % top, axis=1)


def portions_of(count, total, bound, slope, full):
    loads = [(1 << 20) // math.isqrt(grade ** slope) + 1 for grade in range(1, count + 1)]
    largest = bound if full else min(bound, max(-(-total // count), total * loads[0] // sum(loads)))
    least = 1 if total - largest >= count - 1 else 0
    holding, spare = [largest] + [least] * (count - 1), total - largest - least * (count - 1)
    while spare > 0:
        movable = [i for i in range(1, count) if holding[i] < largest] or [i for i in range(1, count) if holding[i] < bound]
        pool, budget = sum([loads[i] for i in movable]), spare
        for i in movable:
            extra = min(bound - holding[i], max(1, budget * loads[i] // pool), spare)
            holding[i] = holding[i] + extra
            spare = spare - extra
    return np.array(holding)


def scatter_about(stream_key, shape, spread, bound, cuts=(), kind=jnp.bfloat16):
    result = spread * jax.random.normal(stream_key, shape, jnp.float32)
    if cuts:
        result = result * block_levels(stream_key, shape, cuts, -0.22, 0.18)
    return jnp.clip(result, -bound, bound).astype(kind)


def setup_inputs(seed: int = 0) -> dict:
    streams_of = jax.random.split(jax.random.key(seed), 8)
    tokens = scatter_about(streams_of[0], (TOKENS, D), 1.0, 6.0, ((0, 32),))
    cotangent = scatter_about(streams_of[1], (TOKENS, D), 0.2, 1.1953125, ((0, 32),))
    expert_ids_keys = jax.random.split(jax.random.fold_in(streams_of[2], 1), TOKENS // TOK_DEV)
    expert_ids_turns = jax.random.permutation(jax.random.fold_in(streams_of[2], 3), TOKENS // TOK_DEV)
    expert_ids = jax.vmap(lambda own, number: shared_out(jax.random.fold_in(streams_of[2], 2), own, number, TOK_DEV, EXPERTS, TOP, CAP, 2))(expert_ids_keys, expert_ids_turns).reshape((TOKENS, TOP))
    route_weight = jnp.clip(jnp.exp(math.log(0.3) - 2.7080503 * jax.random.uniform(streams_of[3], (TOKENS, TOP), jnp.float32) ** block_levels(streams_of[3], (TOKENS, TOP), ((0, 32),), -0.2, 0.2)), 0.02, 0.3)
    gate_proj = scatter_about(streams_of[4], (EXPERTS, D, FF), D ** -0.5, 0.125, ((0, 8),))
    up_proj = scatter_about(streams_of[5], (EXPERTS, D, FF), D ** -0.5, 0.125, ((0, 8),))
    down_proj = scatter_about(streams_of[6], (EXPERTS, FF, D), FF ** -0.5, 0.3125, ((0, 8),))
    return dict(tokens=tokens, cotangent=cotangent, expert_ids=expert_ids, route_weight=route_weight, gate_proj=gate_proj, up_proj=up_proj, down_proj=down_proj)


def expert_block(input_rows, grad_rows, gate_weight, up_weight, down_weight):
    gate_pre = jnp.dot(input_rows, gate_weight, preferred_element_type=jnp.float32)
    up_pre = jnp.dot(input_rows, up_weight, preferred_element_type=jnp.float32)
    gate_sig = jax.nn.sigmoid(gate_pre)
    hidden = (gate_pre * gate_sig * up_pre).astype(jnp.bfloat16)
    expert_out = jnp.dot(hidden, down_weight, preferred_element_type=jnp.float32).astype(jnp.bfloat16)
    hidden_delta = jnp.dot(grad_rows, down_weight.T, preferred_element_type=jnp.float32)
    gate_delta = (hidden_delta * up_pre * gate_sig * (1.0 + gate_pre * (1.0 - gate_sig))).astype(jnp.bfloat16)
    up_delta = (hidden_delta * gate_pre * gate_sig).astype(jnp.bfloat16)
    grad_down = jnp.dot(hidden.T, grad_rows, preferred_element_type=jnp.float32)
    grad_gate = jnp.dot(input_rows.T, gate_delta, preferred_element_type=jnp.float32)
    grad_up = jnp.dot(input_rows.T, up_delta, preferred_element_type=jnp.float32)
    return expert_out, grad_gate, grad_up, grad_down


def reference(tokens, cotangent, expert_ids, route_weight, gate_proj, up_proj, down_proj):
    group_tokens = N_EXPERT * TOK_DEV
    slot_rows = N_EXPERT * CAP
    flat_ids = expert_ids.reshape(N_DP, group_tokens * TOP)
    flat_weight = route_weight.reshape(N_DP, group_tokens * TOP)

    def per_expert(running, expert):
        mixed_sum, route_sum = running

        def per_group(group_index):
            matches = flat_ids[group_index] == expert
            picked = jnp.nonzero(matches, size=slot_rows, fill_value=0)[0].astype(jnp.int32)
            live_count = jnp.sum(matches.astype(jnp.int32))
            live_mask = jnp.arange(slot_rows, dtype=jnp.int32) < live_count
            token_row = (group_index * group_tokens + picked // TOP).astype(jnp.int32)
            input_rows = jnp.where(live_mask[:, None], tokens[token_row], jnp.zeros((), tokens.dtype))
            live_weight = jnp.where(live_mask, flat_weight[group_index, picked], jnp.zeros((), jnp.float32))
            cot_rows = cotangent[token_row]
            grad_rows = (live_weight[:, None] * cot_rows.astype(jnp.float32)).astype(jnp.bfloat16)
            expert_out, grad_gate, grad_up, grad_down = expert_block(
                input_rows, grad_rows, gate_proj[expert], up_proj[expert], down_proj[expert])
            route_part = jnp.sum(cot_rows.astype(jnp.float32) * expert_out.astype(jnp.float32), axis=1)
            route_part = jnp.where(live_mask, route_part, jnp.zeros((), jnp.float32))
            return (token_row, picked, live_weight, expert_out, route_part,
                    grad_gate.astype(jnp.bfloat16), grad_up.astype(jnp.bfloat16), grad_down.astype(jnp.bfloat16))

        token_row, picked, live_weight, expert_out, route_part, gate_parts, up_parts, down_parts = lax.map(
            per_group, jnp.arange(N_DP, dtype=jnp.int32))
        contrib = live_weight[..., None] * expert_out.astype(jnp.float32)
        mixed_sum = mixed_sum.at[token_row.reshape(-1)].add(contrib.reshape(-1, D))
        group_rows = jnp.broadcast_to(jnp.arange(N_DP, dtype=jnp.int32)[:, None], picked.shape)
        route_sum = route_sum.at[group_rows, picked].add(route_part)
        grad_parts = (jnp.sum(gate_parts.astype(jnp.float32), axis=0).astype(jnp.bfloat16),
                      jnp.sum(up_parts.astype(jnp.float32), axis=0).astype(jnp.bfloat16),
                      jnp.sum(down_parts.astype(jnp.float32), axis=0).astype(jnp.bfloat16))
        return (mixed_sum, route_sum), grad_parts

    start_state = (jnp.zeros((TOKENS, D), jnp.float32), jnp.zeros((N_DP, group_tokens * TOP), jnp.float32))
    (mixed_sum, route_sum), (gate_grad, up_grad, down_grad) = lax.scan(
        per_expert, start_state, jnp.arange(EXPERTS, dtype=jnp.int32))
    return (mixed_sum.astype(jnp.bfloat16), route_sum.reshape(TOKENS, TOP), gate_grad, up_grad, down_grad)
```

```python
import jax
import jax.numpy as jnp
from jax import lax
from jax.sharding import PartitionSpec as P

F32 = jnp.float32
BF16 = jnp.bfloat16


def exchange(value, bit):
    return lax.ppermute(value, "expert", [(i, i ^ bit) for i in range(lax.axis_size("expert"))])


def swap_plane(value):
    return lax.ppermute(value, "dp", [(i, i ^ 2) for i in range(4)])


def after(value, *others):
    return lax.optimization_barrier((value,) + others)[0]


def gather_plane(block, gate=None):
    if gate is not None:
        block = after(block, *gate)
    from_x, from_y = exchange(block, 2), exchange(block, 4)
    half = block.shape[0] // 2
    diagonal = [exchange(from_y[:half], 2), exchange(from_x[half:], 4)]
    mine = jnp.concatenate([block, from_x, from_y] + diagonal, axis=0)
    other = exchange(mine, 1)
    return jnp.concatenate([mine, other], axis=0), (from_x[:8, :128], from_y[:8, :128])


OFFSETS = (0, 2, 4, 6, 1, 3, 5, 7)


def dot(a, b, ca, cb):
    return lax.dot_general(a, b, (((ca,), (cb,)), ((), ())), preferred_element_type=F32)


def plane_shards(tokens, cotangent, expert_ids, route_weight, gate_proj, up_proj, down_proj):
    plane, place = lax.axis_index("dp"), lax.axis_index("expert")
    side = plane // 2
    at_end = (plane == 0) | (plane == 3)
    rows, width = tokens.shape
    experts = gate_proj.shape[0] * lax.axis_size("expert")
    hidden_units = gate_proj.shape[2]
    quarter = width // 4
    expert = 2 * place + side
    gate_w = lax.dynamic_index_in_dim(gate_proj, side, 0, False)
    up_w = lax.dynamic_index_in_dim(up_proj, side, 0, False)
    down_w = lax.dynamic_index_in_dim(down_proj, side, 0, False)

    ids_t, weight_t = expert_ids.T, route_weight.T
    chosen = ids_t[:, None, :] == jnp.arange(experts, dtype=jnp.int32)[None, :, None]
    dense = jnp.sum(jnp.where(chosen, weight_t[:, None, :], 0.0), axis=0)[None]
    for bit in (1, 2, 4):
        dense = jnp.concatenate([dense, exchange(dense, bit)], axis=0)
    dense = jnp.concatenate([dense, swap_plane(dense)], axis=0)
    mine = lax.dynamic_index_in_dim(dense, expert, 1, False)
    weights = [
        jnp.concatenate([mine[8 * group + o] for o in OFFSETS])[:, None] for group in range(2)
    ]

    far_tokens = swap_plane(tokens)
    far_cotangent = swap_plane(after(cotangent, far_tokens[:8, :128]))
    xs, cs = [None, None], [None, None]
    xs[0], gate = gather_plane(tokens)
    cs[0], gate = gather_plane(cotangent, gate)
    xs[1], gate = gather_plane(far_tokens, gate)
    cs[1], gate = gather_plane(far_cotangent, gate)

    outs, routes, grads = [], [], None
    for x, c, w in zip(xs, cs, weights):
        gate_pre, up_pre = dot(x, gate_w, 1, 0), dot(x, up_w, 1, 0)
        sig = jax.nn.sigmoid(gate_pre)
        act = gate_pre * sig
        hidden = (act * up_pre).astype(BF16)
        delta = dot(c, down_w, 1, 1)
        routes.append(jnp.sum(hidden.astype(F32) * delta, axis=1))
        delta = w * delta
        gate_delta = (delta * up_pre * sig * (1.0 + gate_pre * (1.0 - sig))).astype(BF16)
        up_delta = (delta * act).astype(BF16)
        weighted = (w * hidden.astype(F32)).astype(BF16)
        outs.append(dot(weighted, down_w, 1, 0).astype(BF16))
        parts = (dot(x, gate_delta, 0, 0), dot(x, up_delta, 0, 0), dot(weighted, c, 0, 0))
        grads = parts if grads is None else tuple(a + b for a, b in zip(grads, parts))
    grads = [g.astype(BF16) for g in grads]

    def piece(array, axis, number):
        return lax.dynamic_slice_in_dim(array, number * quarter, quarter, axis)

    def add(a, b):
        return (a.astype(F32) + b.astype(F32)).astype(BF16)

    inward = [(0, 1), (3, 2)]
    first = jnp.where(at_end, 3 - plane, jnp.where(plane == 1, 0, 3))
    far = jnp.where(plane < 2, 3, 0)
    middle = jnp.where(plane < 2, 2, 1)
    near = jnp.where(plane < 2, 1, 2)
    results = []
    sent = []
    for array, axis in zip(grads, (0, 0, 1)):
        one = lax.ppermute(piece(array, axis, first), "dp", [(0, 1), (1, 0), (2, 3), (3, 2)])
        two = lax.ppermute(piece(array, axis, middle), "dp", inward)
        three = lax.ppermute(piece(array, axis, near), "dp", inward)
        far_sum = lax.ppermute(add(one, piece(array, axis, far)), "dp", [(1, 3), (2, 0)])
        middle_sum = lax.ppermute(add(two, piece(array, axis, middle)), "dp", [(1, 2), (2, 1)])
        own = add(piece(array, axis, plane), jnp.where(at_end, one, three))
        other = jnp.where(at_end, far_sum, middle_sum)
        results.append(
            jnp.stack([jnp.where(side == 0, own, other), jnp.where(side == 0, other, own)])
        )

    outs = jnp.stack(outs).reshape(2, 8, rows, width)
    sums = add(outs[:, :4], exchange(outs[:, 4:], 1))
    half = width // 2
    left, right = sums[..., :half], sums[..., half:]
    left = add(left[:, 0::2], exchange(left[:, 1::2], 2))
    left = add(left[:, 0], exchange(left[:, 1], 4))
    right = add(right[:, :2], exchange(right[:, 2:], 4))
    right = add(right[:, 0], exchange(right[:, 1], 2))
    total = jnp.concatenate([left, right], axis=-1)
    layer_out = add(total[0], swap_plane(total[1]))

    table = jnp.stack(routes).reshape(2, 8, rows)
    table = table[:, [OFFSETS.index(o) for o in range(8)]].reshape(2, 2, 2, 2, 1, rows)
    table = jnp.stack([table[:, :, :, 0], exchange(table[:, :, :, 1], 1)], axis=-2)
    table = jnp.stack([table[:, :, 0], exchange(table[:, :, 1], 2)], axis=-3)
    table = jnp.stack([table[:, 0], exchange(table[:, 1], 4)], axis=-4)
    table = jnp.stack([table[0], swap_plane(table[1])], axis=0).reshape(16, rows)
    source = ((ids_t & 1) ^ side) * 8 + ((ids_t >> 1) ^ place)
    found = source[:, None, :] == jnp.arange(16, dtype=jnp.int32)[None, :, None]
    route_grad = jnp.sum(jnp.where(found, table[None], 0.0), axis=1).T
    return (layer_out, route_grad, *results)


def forward_rows(input_rows, gate_weight, up_weight, down_weight):
    gate_pre = jnp.dot(input_rows, gate_weight, preferred_element_type=jnp.float32)
    up_pre = jnp.dot(input_rows, up_weight, preferred_element_type=jnp.float32)
    gate_sig = jax.nn.sigmoid(gate_pre)
    hidden = (gate_pre * gate_sig * up_pre).astype(jnp.bfloat16)
    expert_out = jnp.dot(hidden, down_weight, preferred_element_type=jnp.float32).astype(
        jnp.bfloat16
    )
    return (gate_pre, up_pre, gate_sig, hidden, expert_out)


def backward_rows(input_rows, grad_rows, kept_state, down_weight):
    gate_pre = kept_state[0]
    up_pre = kept_state[1]
    gate_sig = kept_state[2]
    hidden = kept_state[3]
    hidden_delta = lax.dot_general(
        grad_rows, down_weight, (((1,), (1,)), ((), ())), preferred_element_type=jnp.float32
    )
    gate_delta = (hidden_delta * up_pre * gate_sig * (1.0 + gate_pre * (1.0 - gate_sig))).astype(
        jnp.bfloat16
    )
    up_delta = (hidden_delta * gate_pre * gate_sig).astype(jnp.bfloat16)
    inner = (((0,), (0,)), ((), ()))
    grad_gate = lax.dot_general(input_rows, gate_delta, inner, preferred_element_type=jnp.float32)
    grad_up = lax.dot_general(input_rows, up_delta, inner, preferred_element_type=jnp.float32)
    grad_down = lax.dot_general(hidden, grad_rows, inner, preferred_element_type=jnp.float32)
    return (grad_gate, grad_up, grad_down)


def shards(tokens, cotangent, expert_ids, route_weight, gate_proj, up_proj, down_proj):
    expert_devices = lax.axis_size("expert")
    token_count, model_width = tokens.shape
    per_token = expert_ids.shape[1]
    local_experts = gate_proj.shape[0]
    experts = local_experts * expert_devices
    capacity = token_count * per_token * 5 // (4 * experts)
    total_slots = experts * capacity
    slot_rows = expert_devices * capacity
    flat_ids = expert_ids.reshape(-1)
    pair_count = flat_ids.shape[0]
    matches = flat_ids[:, None] == jnp.arange(experts, dtype=jnp.int32)[None, :]
    onehot = matches.astype(jnp.bfloat16)
    pair_index = jnp.arange(pair_count, dtype=jnp.int32)
    lower = (pair_index[None, :] < pair_index[:, None]).astype(jnp.bfloat16)
    before = jnp.dot(lower, onehot, preferred_element_type=jnp.float32)
    rank = jnp.sum(jnp.where(matches, before, jnp.zeros((), jnp.float32)), axis=1).astype(jnp.int32)
    slot_index = flat_ids * capacity + rank
    owner_row = pair_index // per_token
    slot_token = jnp.zeros((total_slots,), jnp.int32).at[slot_index].set(owner_row)
    slot_weight = (
        jnp.zeros((total_slots,), jnp.float32).at[slot_index].set(route_weight.reshape(-1))
    )
    filled = jnp.zeros((total_slots,), jnp.bool_).at[slot_index].set(True)
    layout = (expert_devices, local_experts, capacity, model_width)
    sent_tokens = jnp.where(
        filled[:, None], tokens[slot_token], jnp.zeros((), jnp.bfloat16)
    ).reshape(layout)
    sent_grads = (slot_weight[:, None] * cotangent[slot_token].astype(jnp.float32)).astype(
        jnp.bfloat16
    )
    sent_grads = sent_grads.reshape(layout)

    def expert_rows(arrived, index_local):
        return arrived[:, index_local].reshape(slot_rows, model_width)

    def send_back(output_list):
        stacked_out = jnp.stack(
            [member.reshape(expert_devices, capacity, model_width) for member in output_list],
            axis=1,
        )
        arrived_out = lax.all_to_all(stacked_out, "expert", split_axis=0, concat_axis=0, tiled=True)
        return arrived_out.reshape(total_slots, model_width)

    output_list = []
    grad_list = []
    arrived_tokens = lax.all_to_all(sent_tokens, "expert", split_axis=0, concat_axis=0, tiled=True)
    states = []
    for index_local in range(local_experts):
        input_rows = expert_rows(arrived_tokens, index_local)
        kept_state = forward_rows(
            input_rows, gate_proj[index_local], up_proj[index_local], down_proj[index_local]
        )
        states.append(kept_state)
        output_list.append(kept_state[4])
    returned = send_back(output_list)
    arrived_grads = lax.all_to_all(sent_grads, "expert", split_axis=0, concat_axis=0, tiled=True)
    for index_local in range(local_experts):
        input_rows = expert_rows(arrived_tokens, index_local)
        grad_list.append(
            backward_rows(
                input_rows,
                expert_rows(arrived_grads, index_local),
                states[index_local],
                down_proj[index_local],
            )
        )
    stacked = tuple((jnp.stack([triple[member] for triple in grad_list]) for member in range(3)))
    reduced = (
        lax.psum_scatter(
            stacked[0].astype(jnp.bfloat16), "dp", scatter_dimension=1, tiled=True
        ).astype(jnp.float32),
        lax.psum_scatter(
            stacked[1].astype(jnp.bfloat16), "dp", scatter_dimension=1, tiled=True
        ).astype(jnp.float32),
        lax.psum_scatter(
            stacked[2].astype(jnp.bfloat16), "dp", scatter_dimension=2, tiled=True
        ).astype(jnp.float32),
    )
    gate_grad = reduced[0].astype(jnp.bfloat16)
    up_grad = reduced[1].astype(jnp.bfloat16)
    down_grad = reduced[2].astype(jnp.bfloat16)
    routed_out = returned[slot_index].reshape(token_count, per_token, model_width)
    layer_out = jnp.sum(route_weight[:, :, None] * routed_out.astype(jnp.float32), axis=1).astype(
        jnp.bfloat16
    )
    route_grad = jnp.einsum("td,tkd->tk", cotangent, routed_out, preferred_element_type=jnp.float32)
    return (layer_out, route_grad, gate_grad, up_grad, down_grad)


def solution(mesh):
    in_specs = (
        P(("dp", "expert"), None),
        P(("dp", "expert"), None),
        P(("dp", "expert"), None),
        P(("dp", "expert"), None),
        P("expert", None, None),
        P("expert", None, None),
        P("expert", None, None),
    )
    out_specs = (
        P(("dp", "expert"), None),
        P(("dp", "expert"), None),
        P("expert", "dp", None),
        P("expert", "dp", None),
        P("expert", None, "dp"),
    )
    small = mesh.shape["dp"] == 4 and mesh.shape["expert"] == 8
    return jax.shard_map(plane_shards if small else shards, mesh=mesh, in_specs=in_specs, out_specs=out_specs, check_vma=False)
```
